32 devices in a mesh: ctx: 2 (over x), fsdp: 16 (over z, y, core).
Axes of the slice: x: 2, y: 2, z: 4, core: 2. Of those that a mesh axis runs over, the one named last changes fastest.
Arguments:
- inputs: bfloat16 [8192, 2048], P(('ctx', 'fsdp')), may hold values from -6 to 6
- cotangent: bfloat16 [8192, 2048], P(('ctx', 'fsdp')), may hold values from -6 to 6
- segment_ids: int32 [4, 2048], replicated, may hold values from 0 to 2, never falling along the last dimension, each value on 1 to 1536 neighbouring positions
- pad_mask: int32 [4, 2048], replicated, may hold values from 0 to 1, as said below
- block_index: int32 [4, 16], replicated, may hold values from 0 to 15, as said below
- attn_norm: bfloat16 [2048], P('fsdp'), may hold values from 0.25 to 1.75
- w_qkv: bfloat16 [2048, 1920], P('fsdp'), may hold values from -0.125 to 0.125
- q_gain: bfloat16 [64], P('fsdp'), may hold values from 0.59765625 to 1.796875
- k_gain: bfloat16 [64], P('fsdp'), may hold values from 0.59765625 to 1.796875
- w_out: bfloat16 [1280, 2048], P('fsdp'), may hold values from -1.25 to 1.25
- ffn_norm: bfloat16 [2048], P('fsdp'), may hold values from 0.25 to 1.75
- w_gate: bfloat16 [2048, 5120], P('fsdp'), may hold values from -0.125 to 0.125
- w_up: bfloat16 [2048, 5120], P('fsdp'), may hold values from -0.125 to 0.125
- w_down: bfloat16 [5120, 2048], P('fsdp'), may hold values from -0.078125 to 0.078125
Outputs:
- output: bfloat16 [8192, 2048], P(('ctx', 'fsdp'))
- input_grad: bfloat16 [8192, 2048], P(('ctx', 'fsdp'))
- attn_norm_grad: float32 [2048], P('fsdp')
- qkv_grad: float32 [2048, 1920], P('fsdp')
- q_gain_grad: float32 [64], P('fsdp')
- k_gain_grad: float32 [64], P('fsdp')
- out_grad: float32 [1280, 2048], P('fsdp')
- ffn_norm_grad: float32 [2048], P('fsdp')
- gate_grad: float32 [2048, 5120], P('fsdp')
- up_grad: float32 [2048, 5120], P('fsdp')
- down_grad: float32 [5120, 2048], P('fsdp')
The draws below stay inside these ranges and needn't reach their ends.
Inputs may be any that keep to these rules, and one draw needn't show every extreme that they name: `segment_ids`: document numbers never fall along the positions of a sequence; each of a sequence's three documents has 1 to 1536 positions, and one has exactly 1536. `pad_mask`: in each sequence the ones form a prefix of 3/4 of its 2048 positions or more, and at least its last position is padding. `block_index`: each row is a permutation of the 16 blocks of 128 positions; entries 2r and 2r + 1 are the blocks stored, in that order, by rank r of the sequence, and they are b and 15 - b for some b.
All inputs are finite; a program needn't handle non-finite values.
Results may differ from the reference program's by a relative error of at most 0.025.
Values may be sent and summed in bfloat16 or wider, within the bound.
No kernel may reach another device: no remote copies, remote signals or barrier semaphores. Data moves between devices by JAX's collectives and lax.ppermute only.
A program may use at most 384 MiB of HBM per device.

```python
import math
import jax
import jax.numpy as jnp
import numpy as np
from jax import lax

D = 2048
HQ = 20
HK = 5
HEAD = 64
FF = 5120
WINDOW = 1024
MEMBERS = 4
TOK_DEV = 256
LENGTH = 2048
BLOCKS = 16
SEQS = 4
TOKENS = 8192
QKV = 1920
N_CTX = 2


def draw_pad_mask(key, part):
    cut_length = jax.random.randint(key, (SEQS, 1), 1, LENGTH // 4 + 1)
    places = jnp.arange(LENGTH, dtype=jnp.int32)[None, :]
    return (places < LENGTH - cut_length).astype(jnp.int32)


def draw_block_index(key, part):
    streams = jax.random.split(key, 2)
    rank_count = BLOCKS // 2
    row_keys = jax.random.split(streams[0], SEQS)
    pair_order = jax.vmap(lambda row_key: jax.random.permutation(row_key, rank_count))(row_keys).astype(jnp.int32)
    flip_bits = jax.random.randint(streams[1], (SEQS, rank_count), 0, 2)
    first_block = jnp.where(flip_bits == 0, pair_order, BLOCKS - 1 - pair_order)
    second = BLOCKS - 1 - first_block
    return jnp.stack([first_block, second], axis=2).reshape(SEQS, BLOCKS).astype(jnp.int32)


def shard_levels(key, extent, cuts, least, high):
    def one(axis_at, blocks):
        steps = jax.random.uniform(jax.random.fold_in(jax.random.fold_in(key, 6), axis_at), (blocks,), jnp.float32, least / len(cuts), high / len(cuts))
        return jnp.repeat(jnp.exp(steps), extent[axis_at] // blocks).reshape((-1,) + (1,) * (len(extent) - axis_at - 1))

    factor_of = one(*cuts[0])
    for cut in cuts[1:]:
        factor_of = factor_of * one(*cut)
    return factor_of


def length_profile(amount, total, most, skew):
    loads = [(1 << 20) // math.isqrt(rank ** skew) + 1 for rank in range(2, amount + 1)]
    rest, given = total - most - (amount - 1), [1] * (amount - 1)
    while rest > 0:
        candidates = [i for i in range(amount - 1) if given[i] < most]
        pool, remaining = sum([loads[i] for i in candidates]), rest
        for i in candidates:
            extra = min(most - given[i], max(1, remaining * loads[i] // pool), rest)
            given[i] = given[i] + extra
            rest = rest - extra
    return np.array([most] + given)


def ragged(own_key, number_of, total, reach, slope):
    if number_of == 2:
        one = jax.random.randint(own_key, (), max(1, total - reach), min(reach, total - 1) + 1)
        return jnp.stack([one, total - one])
    tallies = jnp.asarray(length_profile(number_of, total, reach, slope), jnp.int32)
    couples = (number_of - 1) // 2
    source_of, receiver = tallies[1:1 + 2 * couples:2], tallies[2:2 + 2 * couples:2]
    slack = jnp.minimum(source_of - 1, reach - receiver)
    passed = jax.random.randint(jax.random.fold_in(own_key, 1), (couples,), 0, 1 << 20) % (slack + 1)
    tallies = tallies.at[1:1 + 2 * couples:2].set(source_of - passed).at[2:2 + 2 * couples:2].set(receiver + passed)
    return tallies[jax.random.permutation(jax.random.fold_in(own_key, 2), number_of)]


def normal_values(key, dims, scale, bound, cuts=(), held_as=jnp.bfloat16):
    values = jax.random.normal(key, dims, jnp.float32) * scale
    if len(cuts) > 0:
        values = shard_levels(key, dims, cuts, -0.22, 0.18) * values
    return jnp.clip(values, min=-bound, max=bound).astype(held_as)


def setup_inputs(seed: int = 0) -> dict:
    keys = jax.random.split(jax.random.key(seed), 15)
    inputs = normal_values(keys[0], (TOKENS, D), 1.0, 6.0, ((0, 32),))
    cotangent = normal_values(keys[1], (TOKENS, D), 1.0, 6.0, ((0, 32),))
    segment_ids = jax.vmap(lambda own: jnp.searchsorted(jnp.cumsum(ragged(own, 3, LENGTH, 3 * LENGTH // 4, 0)), jnp.arange(LENGTH), side="right"))(jax.random.split(keys[2], SEQS)).reshape((SEQS, LENGTH)).astype(jnp.int32)
    pad_mask = draw_pad_mask(jax.random.fold_in(keys[14], 71), 0)
    block_index = draw_block_index(jax.random.fold_in(keys[14], 71), 0)
    attn_norm = jnp.clip(1.0 + 0.15 * jax.random.normal(keys[5], (D,), jnp.float32), 0.25, 1.75).astype(jnp.bfloat16)
    w_qkv = normal_values(keys[6], (D, QKV), D ** -0.5, 0.125, ((0, 16),))
    q_gain = jnp.clip(jnp.exp(math.log(1.796875) - 1.1007886 * jax.random.uniform(keys[7], (HEAD,), jnp.float32) ** shard_levels(keys[7], (HEAD,), ((0, 16),), -0.2, 0.2)), 0.59765625, 1.796875).astype(jnp.bfloat16)
    k_gain = jnp.clip(jnp.exp(math.log(1.796875) - 1.1007886 * jax.random.uniform(keys[8], (HEAD,), jnp.float32) ** shard_levels(keys[8], (HEAD,), ((0, 16),), -0.2, 0.2)), 0.59765625, 1.796875).astype(jnp.bfloat16)
    w_out = normal_values(keys[9], (HQ * HEAD, D), (HQ * HEAD // 64) ** -0.5, 1.25, ((0, 16),))
    ffn_norm = jnp.clip(1.0 + 0.15 * jax.random.normal(keys[10], (D,), jnp.float32), 0.25, 1.75).astype(jnp.bfloat16)
    w_gate = normal_values(keys[11], (D, FF), D ** -0.5, 0.125, ((0, 16),))
    w_up = normal_values(keys[12], (D, FF), D ** -0.5, 0.125, ((0, 16),))
    w_down = normal_values(keys[13], (FF, D), FF ** -0.5, 0.078125, ((0, 16),))
    return dict(inputs=inputs, cotangent=cotangent, segment_ids=segment_ids, pad_mask=pad_mask, block_index=block_index, attn_norm=attn_norm, w_qkv=w_qkv, q_gain=q_gain, k_gain=k_gain, w_out=w_out, ffn_norm=ffn_norm, w_gate=w_gate, w_up=w_up, w_down=w_down)


EPSILON = 1e-06
MASKED = -1e+30
ROPE_BASE = 10000.0
HIGHEST = lax.Precision.HIGHEST

@jax.custom_vjp
def low(v):
    return lax.optimization_barrier(v.astype(jnp.bfloat16)).astype(jnp.float32)

@jax.custom_vjp
def low_back(v):
    return v

def low_keep(v):
    return (low(v), None)

def low_pass(kept, grad):
    return (grad,)

def back_keep(v):
    return (v, None)

def back_low(kept, grad):
    return (low(grad),)
low.defvjp(low_keep, low_pass)
low_back.defvjp(back_keep, back_low)

def inverse_rms(values):
    return lax.rsqrt(lax.optimization_barrier(jnp.mean(values * values, axis=-1, keepdims=True)) + EPSILON)

def rope_angles(positions, width):
    frequencies = ROPE_BASE ** (-2.0 * jnp.arange(width // 2, dtype=jnp.float32) / width)
    return positions.astype(jnp.float32)[:, None] * frequencies[None, :]

def rotate(values, angles):
    cosine_table = jnp.cos(angles)[:, None, :]
    sine_table = jnp.sin(angles)[:, None, :]
    half_width = values.shape[-1] // 2
    first_half = values[..., :half_width]
    second_half = values[..., half_width:]
    return jnp.concatenate([first_half * cosine_table - second_half * sine_table, second_half * cosine_table + first_half * sine_table], axis=-1)

def layer(inputs, positions, segments, valid_keys, attn_norm, w_qkv, q_gain, k_gain, w_out, ffn_norm, w_gate, w_up, w_down):
    length = inputs.shape[0]
    group_size = HQ // HK
    normed = low(inputs * inverse_rms(inputs) * attn_norm)
    projected = low_back(jnp.dot(normed, w_qkv, precision=HIGHEST))
    query_raw = projected[:, :HQ * HEAD].reshape(length, HQ, HEAD)
    key_raw = projected[:, HQ * HEAD:(HQ + HK) * HEAD].reshape(length, HK, HEAD)
    value_heads = low(projected[:, (HQ + HK) * HEAD:].reshape(length, HK, HEAD))
    angles = rope_angles(positions, HEAD)
    queries = low(rotate(query_raw * inverse_rms(query_raw) * q_gain, angles)).reshape(length, HK, group_size, HEAD)
    key_heads = low(rotate(key_raw * inverse_rms(key_raw) * k_gain, angles))
    scores = low_back(jnp.einsum('qhgd,khd->hgqk', queries, key_heads, precision=HIGHEST) * HEAD ** (-0.5))
    distance = positions[:, None] - positions[None, :]
    allowed = (distance >= 0) & (distance < WINDOW) & (segments[:, None] == segments[None, :]) & ((valid_keys[None, :] == 1) | (distance == 0))
    scores = jnp.where(allowed, scores, MASKED)
    weights = jnp.exp(scores - lax.optimization_barrier(jnp.max(scores, axis=-1, keepdims=True)))
    probabilities = low(weights / lax.optimization_barrier(jnp.sum(weights, axis=-1, keepdims=True)))
    mixed_heads = jnp.einsum('hgqk,khd->qhgd', probabilities, value_heads, precision=HIGHEST).reshape(length, HQ * HEAD)
    mixed_heads = low(low_back(mixed_heads))
    residual = inputs + low_back(jnp.dot(mixed_heads, w_out, precision=HIGHEST))
    normed_ffn = low(residual * inverse_rms(residual) * ffn_norm)
    gate_pre = low_back(jnp.dot(normed_ffn, w_gate, precision=HIGHEST))
    up_pre = low_back(jnp.dot(normed_ffn, w_up, precision=HIGHEST))
    hidden = low(jax.nn.silu(gate_pre) * up_pre)
    return residual + jnp.dot(hidden, w_down, precision=HIGHEST)

def reference(inputs, cotangent, segment_ids, pad_mask, block_index, attn_norm, w_qkv, q_gain, k_gain, w_out, ffn_norm, w_gate, w_up, w_down):
    half_rows = TOK_DEV // 2

    def to_sequences(stacked):
        return stacked.astype(jnp.float32).reshape(N_CTX, SEQS, MEMBERS, TOK_DEV, D).transpose(1, 0, 2, 3, 4).reshape(SEQS, LENGTH, D)

    def from_sequences(stacked):
        return stacked.reshape(SEQS, N_CTX, MEMBERS, TOK_DEV, D).transpose(1, 0, 2, 3, 4).reshape(TOKENS, D)
    offsets = jnp.arange(half_rows, dtype=jnp.int32)
    positions = (block_index[:, :, None] * half_rows + offsets[None, None, :]).reshape(SEQS, LENGTH).astype(jnp.int32)
    segments = jnp.take_along_axis(segment_ids, positions, axis=1)
    valid_keys = jnp.take_along_axis(pad_mask, positions, axis=1)
    params = (attn_norm.astype(jnp.float32), w_qkv.astype(jnp.float32), q_gain.astype(jnp.float32), k_gain.astype(jnp.float32), w_out.astype(jnp.float32), ffn_norm.astype(jnp.float32), w_gate.astype(jnp.float32), w_up.astype(jnp.float32), w_down.astype(jnp.float32))
    layer_step = jax.checkpoint(layer)

    def forward(sequences, *weights):

        def scan_step(scan_carry, scan_item):
            return (scan_carry, layer_step(scan_item[0], scan_item[1], scan_item[2], scan_item[3], *weights))
        return lax.scan(scan_step, None, (sequences, positions, segments, valid_keys))[1]
    result, pullback = jax.vjp(forward, to_sequences(inputs), *params)
    gradients = pullback(to_sequences(cotangent))
    return (from_sequences(result).astype(jnp.bfloat16), from_sequences(gradients[0]).astype(jnp.bfloat16), gradients[1], gradients[2], gradients[3], gradients[4], gradients[5], gradients[6], gradients[7], gradients[8], gradients[9])
```

```python
import jax
import jax.numpy as jnp
from jax import lax
from jax.sharding import PartitionSpec as P

HQ = 20
HK = 5
HEAD = 64
WINDOW = 1024
MEMBERS = 4


EPSILON = 1e-06
MASKED = -1e30
ROPE_BASE = 10000.0


SEQUENCE = ("x", "y", "c")
MEMBER = ("y", "c")
FSDP = ("z", "y", "c")


def swapped(array, axis):
    return lax.ppermute(array, axis, [(0, 1), (1, 0)])


def plane_gather(block):
    half = block.shape[0] // 2
    by_x = swapped(block, "x")
    by_y = swapped(block, "y")
    by_c = swapped(block, "c")
    far = jnp.concatenate([swapped(by_x[:half], "y"), swapped(by_y[half:], "x")], axis=0)
    return [
        block,
        by_c,
        by_y,
        swapped(by_y, "c"),
        by_x,
        swapped(by_x, "c"),
        far,
        swapped(far, "c"),
    ]


def added(one, other):
    return one.astype(jnp.float32) + other.astype(jnp.float32)


def plane_scatter(terms):
    terms = terms.astype(jnp.bfloat16)
    half = terms.shape[1] // 2
    pairs = terms.reshape(4, 2, *terms.shape[1:])
    chip = added(pairs[:, 0], swapped(pairs[:, 1], "c")).astype(jnp.bfloat16)
    first, second = chip[:, :half], chip[:, half:]
    got_x = swapped(first[2:], "x")
    got_y = swapped(second[1::2], "y")
    first = added(first[:2], got_x)
    second = added(second[::2], got_y)
    last_y = swapped(first[1].astype(jnp.bfloat16), "y")
    last_x = swapped(second[1].astype(jnp.bfloat16), "x")
    return jnp.concatenate([added(first[0], last_y), added(second[0], last_x)], axis=0)


def sum_everywhere(value):
    for axis in SEQUENCE:
        value = value + swapped(value, axis)
    size = lax.axis_size("z")
    shift = 1
    while shift < size:
        value = value + lax.ppermute(value, "z", [(i, i ^ shift) for i in range(size)])
        shift *= 2
    return value


def inverse_rms(values):
    return lax.rsqrt(jnp.mean(values * values, axis=-1, keepdims=True) + EPSILON)


def rope_angles(positions, width):
    frequencies = ROPE_BASE ** (-2.0 * jnp.arange(width // 2, dtype=jnp.float32) / width)
    return positions.astype(jnp.float32)[:, None] * frequencies[None, :]


def rotate(values, angles):
    cosine_table = jnp.cos(angles)[:, None, :]
    sine_table = jnp.sin(angles)[:, None, :]
    half_width = values.shape[-1] // 2
    first_half = values[..., :half_width]
    second_half = values[..., half_width:]
    return jnp.concatenate(
        [
            first_half * cosine_table - second_half * sine_table,
            second_half * cosine_table + first_half * sine_table,
        ],
        axis=-1,
    )


def rotate_back(values, angles):
    cosine_table = jnp.cos(angles)[:, None, :]
    sine_table = jnp.sin(angles)[:, None, :]
    half_width = values.shape[-1] // 2
    first_half = values[..., :half_width]
    second_half = values[..., half_width:]
    return jnp.concatenate(
        [
            first_half * cosine_table + second_half * sine_table,
            second_half * cosine_table - first_half * sine_table,
        ],
        axis=-1,
    )


def norm_back(incoming, values, scale_inv):
    return scale_inv * (
        incoming
        - values * scale_inv * scale_inv * jnp.mean(incoming * values, axis=-1, keepdims=True)
    )


def shards(
    inputs,
    cotangent,
    segment_ids,
    pad_mask,
    block_index,
    attn_norm,
    w_qkv,
    q_gain,
    k_gain,
    w_out,
    ffn_norm,
    w_gate,
    w_up,
    w_down,
):
    f32, bf16 = jnp.float32, jnp.bfloat16
    rows, width = inputs.shape
    half_rows = rows // 2
    group_size = HQ // HK
    head_scale = HEAD ** (-0.5)
    seqs = lax.axis_size("z")
    ctx = lax.axis_index("x")
    member = 2 * lax.axis_index("y") + lax.axis_index("c")
    sequence = lax.axis_index("z")
    rank = MEMBERS * ctx + member

    norm_one = attn_norm.astype(f32)[:, None]
    norm_two = ffn_norm.astype(f32)[:, None]
    weight_qkv = lax.all_gather((w_qkv * norm_one).astype(bf16), FSDP, axis=0, tiled=True)
    gains = lax.all_gather(jnp.stack([q_gain, k_gain]), FSDP, axis=1, tiled=True).astype(f32)
    gain_query, gain_key = gains[0], gains[1]
    part_rows, ff = w_gate.shape
    piece = w_down.shape[0] // 2

    def chosen(weight):
        view = (weight * norm_two).astype(bf16).reshape(part_rows, seqs, MEMBERS, 2, piece)
        mine = lax.dynamic_index_in_dim(view, ctx, 3, keepdims=False)
        return mine.transpose(2, 0, 1, 3).reshape(MEMBERS, part_rows, seqs * piece)

    sent = lax.all_to_all(
        jnp.stack([chosen(w_gate), chosen(w_up)], axis=1),
        MEMBER,
        split_axis=0,
        concat_axis=0,
        tiled=True,
    )
    share = seqs * piece
    weight_gate = lax.all_gather(sent[:, 0].reshape(-1, share), "z", axis=0, tiled=True)
    weight_up = lax.all_gather(sent[:, 1].reshape(-1, share), "z", axis=0, tiled=True)
    weight_down = lax.all_gather(
        lax.dynamic_slice_in_dim(w_down, ctx * piece, piece), "z", axis=0, tiled=True
    )
    weight_out = lax.all_gather(w_out, FSDP, axis=0, tiled=True)

    slots = lax.dynamic_index_in_dim(block_index, sequence, 0, keepdims=False)
    segment_row = lax.dynamic_index_in_dim(segment_ids, sequence, 0, keepdims=False)
    valid_row = lax.dynamic_index_in_dim(pad_mask, sequence, 0, keepdims=False)
    ranks = jnp.bitwise_xor(rank, jnp.arange(2 * MEMBERS, dtype=jnp.int32))
    picked = (2 * ranks[:, None] + jnp.arange(2, dtype=jnp.int32)[None, :]).reshape(-1)
    key_blocks = jnp.take(slots, picked)
    key_positions = (
        key_blocks[:, None] * half_rows + jnp.arange(half_rows, dtype=jnp.int32)[None, :]
    ).reshape(-1)
    key_segments = jnp.take(segment_row.reshape(-1, half_rows), key_blocks, axis=0).reshape(-1)
    key_valid = jnp.take(valid_row.reshape(-1, half_rows), key_blocks, axis=0).reshape(-1)
    query_positions = key_positions[:rows]
    query_segments = key_segments[:rows]
    distance = query_positions[:, None] - key_positions[None, :]
    allowed = (
        (distance >= 0)
        & (distance < WINDOW)
        & (query_segments[:, None] == key_segments[None, :])
        & ((key_valid[None, :] == 1) | (distance == 0))
    )
    angles = rope_angles(query_positions, HEAD)

    x_float = inputs.astype(f32)
    scale_one = inverse_rms(x_float)
    normed = (x_float * scale_one).astype(bf16)
    projected = jnp.dot(normed, weight_qkv, preferred_element_type=f32)
    query_raw = projected[:, : HQ * HEAD].reshape(rows, HQ, HEAD)
    key_raw = projected[:, HQ * HEAD : (HQ + HK) * HEAD].reshape(rows, HK, HEAD)
    value_part = projected[:, (HQ + HK) * HEAD :].astype(bf16)
    query_scale = inverse_rms(query_raw)
    key_scale = inverse_rms(key_raw)
    key_part = (
        rotate(key_raw * key_scale * gain_key, angles).astype(bf16).reshape(rows, HK * HEAD)
    )
    gathered = jnp.concatenate(
        plane_gather(jnp.concatenate([key_part, value_part], axis=1)), axis=0
    )
    queries = rotate(query_raw * query_scale * gain_query, angles).astype(bf16)
    key_heads = gathered[:, : HK * HEAD].reshape(-1, HK, HEAD)
    value_heads = gathered[:, HK * HEAD :].reshape(-1, HK, HEAD)
    query_heads = queries.reshape(rows, HK, group_size, HEAD)
    head_outputs = []
    log_totals = []
    for kv_head in range(HK):
        scores = (
            jnp.einsum(
                "qgd,kd->gqk",
                query_heads[:, kv_head],
                key_heads[:, kv_head],
                preferred_element_type=f32,
            )
            * head_scale
        )
        scores = jnp.where(allowed[None], scores, MASKED)
        row_max = jnp.max(scores, axis=-1, keepdims=True)
        weights = jnp.exp(scores - row_max)
        row_total = jnp.sum(weights, axis=-1, keepdims=True)
        probabilities = (weights / row_total).astype(bf16)
        log_totals.append(row_max + jnp.log(row_total))
        head_outputs.append(
            jnp.einsum(
                "gqk,kd->qgd",
                probabilities,
                value_heads[:, kv_head],
                preferred_element_type=f32,
            )
        )
    mixed = jnp.stack(head_outputs, axis=1).reshape(rows, HQ * HEAD).astype(bf16)
    residual = x_float + jnp.dot(mixed, weight_out, preferred_element_type=f32)
    scale_two = inverse_rms(residual)
    normed_ffn = (residual * scale_two).astype(bf16)

    d_all = jnp.concatenate(plane_gather(cotangent), axis=0)
    n_all = jnp.concatenate(plane_gather(normed_ffn), axis=0)
    d_hidden = jnp.einsum("td,fd->tf", d_all, weight_down, preferred_element_type=f32)
    gate_pre = jnp.dot(n_all, weight_gate, preferred_element_type=f32)
    up_pre = jnp.dot(n_all, weight_up, preferred_element_type=f32)
    gate_sigmoid = jax.nn.sigmoid(gate_pre)
    hidden = (gate_pre * gate_sigmoid * up_pre).astype(bf16)
    d_gate = (d_hidden * up_pre * gate_sigmoid * (1.0 + gate_pre * (1.0 - gate_sigmoid))).astype(
        bf16
    )
    d_up = (d_hidden * gate_pre * gate_sigmoid).astype(bf16)
    d_normed_terms = jnp.einsum(
        "tf,df->td", d_gate, weight_gate, preferred_element_type=f32
    ) + jnp.einsum("tf,df->td", d_up, weight_up, preferred_element_type=f32)
    d_normed_ffn = plane_scatter(d_normed_terms.reshape(2 * MEMBERS, rows, width))
    output_terms = jnp.dot(hidden, weight_down, preferred_element_type=f32)
    output = (residual + plane_scatter(output_terms.reshape(2 * MEMBERS, rows, width))).astype(
        bf16
    )
    down_term = jnp.einsum("tf,td->fd", hidden, d_all, preferred_element_type=f32)
    gate_term = jnp.einsum("td,tf->df", n_all, d_gate, preferred_element_type=f32)
    up_term = jnp.einsum("td,tf->df", n_all, d_up, preferred_element_type=f32)

    def z_sum(term):
        return lax.psum_scatter(term.astype(bf16), "z", scatter_dimension=0, tiled=True)

    down_sum = z_sum(down_term)
    gate_sum = z_sum(gate_term)
    up_sum = z_sum(up_term)

    d_residual = cotangent.astype(f32) + norm_back(d_normed_ffn, residual, scale_two)
    d_attn = d_residual.astype(bf16)
    out_term = jnp.einsum("tc,td->cd", mixed, d_attn, preferred_element_type=f32)
    d_mixed = (
        jnp.einsum("td,cd->tc", d_attn, weight_out, preferred_element_type=f32)
        .astype(bf16)
        .reshape(rows, HK, group_size, HEAD)
    )
    query_grads = []
    key_grads = []
    value_grads = []
    for kv_head in range(HK):
        query_block = query_heads[:, kv_head]
        scores = (
            jnp.einsum(
                "qgd,kd->gqk",
                query_block,
                key_heads[:, kv_head],
                preferred_element_type=f32,
            )
            * head_scale
        )
        scores = jnp.where(allowed[None], scores, MASKED)
        probs_float = jnp.exp(scores - log_totals[kv_head])
        probabilities = probs_float.astype(bf16)
        d_probs = jnp.einsum(
            "qgd,kd->gqk",
            d_mixed[:, kv_head],
            value_heads[:, kv_head],
            preferred_element_type=f32,
        )
        d_scores = (
            probs_float * (d_probs - jnp.sum(probs_float * d_probs, axis=-1, keepdims=True))
        ).astype(bf16)
        query_grads.append(
            jnp.einsum(
                "gqk,kd->qgd", d_scores, key_heads[:, kv_head], preferred_element_type=f32
            )
            * head_scale
        )
        key_grads.append(
            jnp.einsum("gqk,qgd->kd", d_scores, query_block, preferred_element_type=f32)
            * head_scale
        )
        value_grads.append(
            jnp.einsum(
                "gqk,qgd->kd",
                probabilities,
                d_mixed[:, kv_head],
                preferred_element_type=f32,
            )
        )
    d_query = jnp.stack(query_grads, axis=1).reshape(rows, HQ, HEAD)
    kv_terms = jnp.concatenate(
        [
            jnp.stack(key_grads, axis=1).reshape(-1, HK * HEAD),
            jnp.stack(value_grads, axis=1).reshape(-1, HK * HEAD),
        ],
        axis=1,
    )
    d_kv = plane_scatter(kv_terms.reshape(2 * MEMBERS, rows, 2 * HK * HEAD))
    d_key = d_kv[:, : HK * HEAD].reshape(rows, HK, HEAD)
    d_value = d_kv[:, HK * HEAD :]
    d_query_normed = rotate_back(d_query, angles)
    d_key_normed = rotate_back(d_key, angles)
    q_gain_term = jnp.sum(d_query_normed * query_raw * query_scale, axis=(0, 1))
    k_gain_term = jnp.sum(d_key_normed * key_raw * key_scale, axis=(0, 1))
    d_query_raw = norm_back(d_query_normed * gain_query, query_raw, query_scale)
    d_key_raw = norm_back(d_key_normed * gain_key, key_raw, key_scale)
    d_projected = jnp.concatenate(
        [d_query_raw.reshape(rows, HQ * HEAD), d_key_raw.reshape(rows, HK * HEAD), d_value], axis=1
    ).astype(bf16)
    qkv_term = jnp.einsum("td,tc->dc", normed, d_projected, preferred_element_type=f32)
    d_normed = jnp.einsum("tc,dc->td", d_projected, weight_qkv, preferred_element_type=f32)
    input_grad = (d_residual + norm_back(d_normed, x_float, scale_one)).astype(bf16)

    def fsdp_sum(term):
        part = lax.psum_scatter(term.astype(bf16), FSDP, scatter_dimension=0, tiled=True)
        return added(part, swapped(part, "x"))

    def both(mine):
        other = swapped(mine, "x")
        low = jnp.where(ctx == 0, mine, other)
        high = jnp.where(ctx == 0, other, mine)
        return low, high

    def placed(total):
        moved = lax.all_to_all(
            total.reshape(MEMBERS, part_rows, share),
            MEMBER,
            split_axis=0,
            concat_axis=0,
            tiled=True,
        )
        low, high = both(moved)
        whole = jnp.stack([low, high]).reshape(2, MEMBERS, part_rows, seqs, piece)
        return whole.transpose(2, 3, 1, 0, 4).reshape(part_rows, ff).astype(f32)

    gate_raw = placed(gate_sum)
    up_raw = placed(up_sum)
    ffn_norm_grad = jnp.sum(
        gate_raw * w_gate.astype(f32) + up_raw * w_up.astype(f32), axis=1
    )
    down_grad = jnp.concatenate(both(down_sum), axis=0).astype(f32)
    out_grad = fsdp_sum(out_term)
    qkv_raw = fsdp_sum(qkv_term)
    attn_norm_grad = jnp.sum(qkv_raw * w_qkv.astype(f32), axis=1)
    gain_terms = sum_everywhere(jnp.stack([q_gain_term, k_gain_term]))
    gain_width = q_gain.shape[0]
    gain_grads = lax.dynamic_slice_in_dim(
        gain_terms, (sequence * MEMBERS + member) * gain_width, gain_width, axis=1
    )
    return (
        output,
        input_grad,
        attn_norm_grad,
        qkv_raw * norm_one,
        gain_grads[0],
        gain_grads[1],
        out_grad,
        ffn_norm_grad,
        gate_raw * norm_two,
        up_raw * norm_two,
        down_grad,
    )


def solution(mesh):
    fsdp = mesh.shape["fsdp"]
    devices = mesh.devices.reshape(2, fsdp // MEMBERS, 2, 2)
    inner = jax.sharding.Mesh(devices, ("x", "z", "y", "c"))
    tokens = P(("x",) + FSDP, None)
    return jax.shard_map(
        shards,
        mesh=inner,
        in_specs=(
            tokens,
            tokens,
            P(),
            P(),
            P(),
            P(FSDP),
            P(FSDP, None),
            P(FSDP),
            P(FSDP),
            P(FSDP, None),
            P(FSDP),
            P(FSDP, None),
            P(FSDP, None),
            P(FSDP, None),
        ),
        out_specs=(
            tokens,
            tokens,
            P(FSDP),
            P(FSDP, None),
            P(FSDP),
            P(FSDP),
            P(FSDP, None),
            P(FSDP),
            P(FSDP, None),
            P(FSDP, None),
            P(FSDP, None),
        ),
        check_vma=False,
    )
```

```python
import functools

import jax
import jax.numpy as jnp
from jax import lax
from jax.experimental import pallas as pl
from jax.experimental.pallas import tpu as pltpu
from jax.sharding import PartitionSpec as P

HQ = 20
HK = 5
HEAD = 64
WINDOW = 1024
MEMBERS = 4


EPSILON = 1e-06
MASKED = -1e30
LANES = 128
ROPE_BASE = 10000.0


SEQUENCE = ("x", "y", "c")
MEMBER = ("y", "c")
FSDP = ("z", "y", "c")


def swapped(array, axis):
    return lax.ppermute(array, axis, [(0, 1), (1, 0)])


def plane_gather(block):
    half = block.shape[0] // 2
    by_x = swapped(block, "x")
    by_y = swapped(block, "y")
    by_c = swapped(block, "c")
    far = jnp.concatenate([swapped(by_x[:half], "y"), swapped(by_y[half:], "x")], axis=0)
    return [
        block,
        by_c,
        by_y,
        swapped(by_y, "c"),
        by_x,
        swapped(by_x, "c"),
        far,
        swapped(far, "c"),
    ]


def added(one, other):
    return one.astype(jnp.float32) + other.astype(jnp.float32)


def plane_scatter(terms):
    terms = terms.astype(jnp.bfloat16)
    half = terms.shape[1] // 2
    pairs = terms.reshape(4, 2, *terms.shape[1:])
    chip = added(pairs[:, 0], swapped(pairs[:, 1], "c")).astype(jnp.bfloat16)
    first, second = chip[:, :half], chip[:, half:]
    got_x = swapped(first[2:], "x")
    got_y = swapped(second[1::2], "y")
    first = added(first[:2], got_x)
    second = added(second[::2], got_y)
    last_y = swapped(first[1].astype(jnp.bfloat16), "y")
    last_x = swapped(second[1].astype(jnp.bfloat16), "x")
    return jnp.concatenate([added(first[0], last_y), added(second[0], last_x)], axis=0)


def inverse_rms(values):
    return lax.rsqrt(jnp.mean(values * values, axis=-1, keepdims=True) + EPSILON)


def rope_angles(positions, width):
    frequencies = ROPE_BASE ** (-2.0 * jnp.arange(width // 2, dtype=jnp.float32) / width)
    return positions.astype(jnp.float32)[:, None] * frequencies[None, :]


def rotate(values, angles):
    cosine_table = jnp.cos(angles)[:, None, :]
    sine_table = jnp.sin(angles)[:, None, :]
    half_width = values.shape[-1] // 2
    first_half = values[..., :half_width]
    second_half = values[..., half_width:]
    return jnp.concatenate(
        [
            first_half * cosine_table - second_half * sine_table,
            second_half * cosine_table + first_half * sine_table,
        ],
        axis=-1,
    )


def rotate_back(values, angles):
    cosine_table = jnp.cos(angles)[:, None, :]
    sine_table = jnp.sin(angles)[:, None, :]
    half_width = values.shape[-1] // 2
    first_half = values[..., :half_width]
    second_half = values[..., half_width:]
    return jnp.concatenate(
        [
            first_half * cosine_table + second_half * sine_table,
            second_half * cosine_table - first_half * sine_table,
        ],
        axis=-1,
    )


def norm_back(incoming, values, scale_inv):
    return scale_inv * (
        incoming
        - values * scale_inv * scale_inv * jnp.mean(incoming * values, axis=-1, keepdims=True)
    )


def taken(index_ref, half, slots, block, kv_ref):
    parts = []
    for slot in range(slots):
        start = pl.multiple_of(index_ref[half * slots + slot] * block, block)
        parts.append(kv_ref[pl.ds(start, block), :])
    return jnp.concatenate(parts, axis=0)


def grouped(ref, half, block, group):
    wide = ref[pl.ds(half * block, block), :]
    return jnp.concatenate(
        [wide[:, g * HEAD : (g + 1) * HEAD] for g in range(group)], axis=0
    )


def attend_kernel(slots, block, group, index_ref, q_ref, kv_ref, bias_ref, mixed_ref):
    rows = group * block
    for half in range(2):
        pair = taken(index_ref, half, slots, block, kv_ref)
        keys = pair[:, :HEAD]
        lane = lax.broadcasted_iota(jnp.int32, pair.shape, 1)
        values = jnp.where(lane < HEAD, jnp.ones_like(pair), pair)
        query = grouped(q_ref, half, block, group) * jnp.bfloat16(HEAD ** (-0.5))
        scores = lax.dot_general(
            query, keys, (((1,), (1,)), ((), ())), preferred_element_type=jnp.float32
        )
        bias = bias_ref[half]
        weights = jnp.exp(scores + jnp.concatenate([bias] * group, axis=0)).astype(jnp.bfloat16)
        total = jnp.dot(weights, values, preferred_element_type=jnp.float32)
        result = (total[:, HEAD:] / total[:, :HEAD]).astype(jnp.bfloat16)
        for g in range(group):
            mixed_ref[half * block : (half + 1) * block, g * HEAD : (g + 1) * HEAD] = result[
                g * block : (g + 1) * block
            ]


def attend(index, queries, pairs, bias):
    rows = queries.shape[0]
    block = rows // 2
    slots = WINDOW // block + 1
    group = HQ // HK
    wide = group * HEAD
    return pl.pallas_call(
        functools.partial(attend_kernel, slots, block, group),
        grid_spec=pltpu.PrefetchScalarGridSpec(
            num_scalar_prefetch=1,
            grid=(HK,),
            in_specs=[
                pl.BlockSpec((rows, wide), lambda h, index: (0, h)),
                pl.BlockSpec((pairs.shape[0], 2 * HEAD), lambda h, index: (0, h)),
                pl.BlockSpec(bias.shape, lambda h, index: (0, 0, 0)),
            ],
            out_specs=pl.BlockSpec((rows, wide), lambda h, index: (0, h)),
        ),
        out_shape=jax.ShapeDtypeStruct(queries.shape, jnp.bfloat16),
        name="attend",
    )(index, queries, pairs, bias)


def attend_back_kernel(
    slots, block, group, index_ref, q_ref, kv_ref, dm_ref, bias_ref, dq_ref, dkv_ref, sums
):
    scale = jnp.bfloat16(HEAD ** (-0.5))
    sums[...] = jnp.zeros_like(sums)
    nt = (((1,), (1,)), ((), ()))
    for half in range(2):
        pair = taken(index_ref, half, slots, block, kv_ref)
        keys = pair[:, :HEAD]
        values = pair[:, HEAD:]
        query = grouped(q_ref, half, block, group) * scale
        grads = grouped(dm_ref, half, block, group)
        scores = lax.dot_general(keys, query, nt, preferred_element_type=jnp.float32)
        bias = bias_ref[half]
        weights = jnp.exp(scores + jnp.concatenate([bias] * group, axis=1))
        probs = weights * (1.0 / jnp.sum(weights, axis=0, keepdims=True))
        d_probs = lax.dot_general(values, grads, nt, preferred_element_type=jnp.float32)
        delta = jnp.sum(probs * d_probs, axis=0, keepdims=True)
        d_scores = (probs * (d_probs - delta)).astype(jnp.bfloat16)
        d_values = jnp.dot(probs.astype(jnp.bfloat16), grads, preferred_element_type=jnp.float32)
        d_keys = jnp.dot(d_scores, query, preferred_element_type=jnp.float32)
        both = jnp.concatenate([d_keys, d_values], axis=1)
        for slot in range(slots):
            start = pl.multiple_of(index_ref[half * slots + slot] * block, block)
            sums[pl.ds(start, block), :] += both[slot * block : (slot + 1) * block]
        d_query = jnp.dot(
            (keys * scale).T, d_scores, preferred_element_type=jnp.float32
        )
        for g in range(group):
            dq_ref[half * block : (half + 1) * block, g * HEAD : (g + 1) * HEAD] = d_query[
                :, g * block : (g + 1) * block
            ].T
    dkv_ref[...] = sums[...].astype(jnp.bfloat16)


def attend_back(index, queries, pairs, d_mixed, bias):
    rows = queries.shape[0]
    block = rows // 2
    slots = WINDOW // block + 1
    group = HQ // HK
    wide = group * HEAD
    keys = pairs.shape[0]
    return pl.pallas_call(
        functools.partial(attend_back_kernel, slots, block, group),
        grid_spec=pltpu.PrefetchScalarGridSpec(
            num_scalar_prefetch=1,
            grid=(HK,),
            in_specs=[
                pl.BlockSpec((rows, wide), lambda h, index: (0, h)),
                pl.BlockSpec((keys, 2 * HEAD), lambda h, index: (0, h)),
                pl.BlockSpec((rows, wide), lambda h, index: (0, h)),
                pl.BlockSpec(bias.shape, lambda h, index: (0, 0, 0)),
            ],
            out_specs=[
                pl.BlockSpec((rows, wide), lambda h, index: (0, h)),
                pl.BlockSpec((keys, 2 * HEAD), lambda h, index: (0, h)),
            ],
            scratch_shapes=[pltpu.VMEM((keys, 2 * HEAD), jnp.float32)],
        ),
        out_shape=[
            jax.ShapeDtypeStruct(queries.shape, jnp.float32),
            jax.ShapeDtypeStruct(pairs.shape, jnp.bfloat16),
        ],
        name="attend_back",
    )(index, queries, pairs, d_mixed, bias)


def mask_tables(block_index_row, segment_row, valid_row, rank, rows):
    block = rows // 2
    slots = WINDOW // block + 1
    blocks = block_index_row.shape[0]
    own = lax.dynamic_slice_in_dim(block_index_row, 2 * rank, 2)
    wanted = own[:, None] - jnp.arange(slots, dtype=jnp.int32)[None, :]
    there = wanted >= 0
    wanted = jnp.maximum(wanted, 0)
    match = wanted[:, :, None] == block_index_row[None, None, :]
    place = jnp.sum(
        jnp.where(match, jnp.arange(blocks, dtype=jnp.int32)[None, None, :], 0), axis=-1
    )
    index = 2 * jnp.bitwise_xor(place // 2, rank) + place % 2
    segments = segment_row.reshape(blocks, block)
    valid = valid_row.reshape(blocks, block)

    def rows_of(table, at):
        hot = (at[..., None] == jnp.arange(blocks, dtype=jnp.int32)).astype(jnp.float32)
        return jnp.einsum("...b,bj->...j", hot, table.astype(jnp.float32), precision=lax.Precision.HIGHEST)

    own_segments = rows_of(segments, own)
    key_segments = rows_of(segments, wanted)
    key_valid = rows_of(valid, wanted)
    offset = (
        jnp.arange(block, dtype=jnp.int32)[:, None, None]
        - jnp.arange(block, dtype=jnp.int32)[None, None, :]
        + block * jnp.arange(slots, dtype=jnp.int32)[None, :, None]
    )
    allowed = (
        ((offset >= 0) & (offset < WINDOW))[None]
        & there[:, None, :, None]
        & (own_segments[:, :, None, None] == key_segments[:, None])
        & ((key_valid[:, None] == 1.0) | (offset == 0)[None])
    )
    bias = jnp.where(allowed, 0.0, -1e30).astype(jnp.float32).reshape(2, block, slots * block)
    return index.reshape(-1).astype(jnp.int32), bias


def after(value, *others):
    return lax.optimization_barrier((value, *others))[0]


def assemble_kernel(where_ref, *refs):
    *blocks, whole = refs
    half = whole.shape[3] // 2
    for k, block in enumerate(blocks):
        member = jnp.bitwise_xor(where_ref[0], k % MEMBERS)
        start = pl.multiple_of(jnp.bitwise_xor(where_ref[1], k // MEMBERS) * half, LANES)
        whole[:, pl.ds(member, 1), :, pl.ds(start, half)] = block[...][:, None]


def assemble(where, blocks):
    seqs, rows, half = blocks[0].shape
    return pl.pallas_call(
        assemble_kernel,
        in_specs=[pl.BlockSpec(memory_space=pltpu.SMEM)]
        + [pl.BlockSpec(memory_space=pltpu.VMEM)] * len(blocks),
        out_specs=pl.BlockSpec(memory_space=pltpu.VMEM),
        out_shape=jax.ShapeDtypeStruct((seqs, MEMBERS, rows, 2 * half), blocks[0].dtype),
        name="assemble",
    )(where, *blocks)


def split_kernel(where_ref, whole_ref, extra_ref, terms_ref):
    terms_ref[...] = whole_ref[:, 0][None]

    if extra_ref is not None:

        @pl.when(jnp.bitwise_xor(where_ref[1], pl.program_id(0) // MEMBERS) == 1)
        def _():
            shape = terms_ref.shape[:-1] + (LANES,)
            terms_ref[..., terms_ref.shape[-1] - LANES :] = jnp.broadcast_to(
                extra_ref[:, 0][None], shape
            ).astype(terms_ref.dtype)


def split_plain_kernel(where_ref, whole_ref, terms_ref):
    split_kernel(where_ref, whole_ref, None, terms_ref)


def split(where, whole, extra=None):
    seqs, members, rows, columns = whole.shape
    half = columns // 2

    def at(k, where):
        return (
            0,
            jnp.bitwise_xor(where[0], k % MEMBERS),
            0,
            jnp.bitwise_xor(where[1], k // MEMBERS),
        )

    in_specs = [pl.BlockSpec((seqs, 1, rows, half), at)]
    operands = [whole]
    if extra is not None:
        in_specs.append(
            pl.BlockSpec(
                (seqs, 1, 1, LANES),
                lambda k, where: (0, jnp.bitwise_xor(where[0], k % MEMBERS), 0, 0),
            )
        )
        operands.append(extra)
    return pl.pallas_call(
        split_plain_kernel if extra is None else split_kernel,
        grid_spec=pltpu.PrefetchScalarGridSpec(
            num_scalar_prefetch=1,
            grid=(2 * members,),
            in_specs=in_specs,
            out_specs=pl.BlockSpec((1, seqs, rows, half), lambda k, where: (k, 0, 0, 0)),
        ),
        out_shape=jax.ShapeDtypeStruct((2 * members, seqs, rows, half), whole.dtype),
        name="split",
    )(where, *operands)


def assemble_plain(where, blocks):
    order = jnp.bitwise_xor(MEMBERS * where[1] + where[0], jnp.arange(2 * MEMBERS))
    seqs, rows, half = blocks[0].shape
    kept = jnp.take(jnp.stack(blocks), order, axis=0)
    kept = kept.reshape(2, MEMBERS, seqs, rows, half)
    return kept.transpose(2, 1, 3, 0, 4).reshape(seqs, MEMBERS, rows, 2 * half)


def split_plain(where, whole):
    order = jnp.bitwise_xor(MEMBERS * where[1] + where[0], jnp.arange(2 * MEMBERS))
    seqs, members, rows, columns = whole.shape
    parts = whole.reshape(seqs, members, rows, 2, columns // 2).transpose(3, 1, 0, 2, 4)
    return jnp.take(parts.reshape(2 * members, seqs, rows, columns // 2), order, axis=0)


def shards(
    inputs,
    cotangent,
    segment_ids,
    pad_mask,
    block_index,
    attn_norm,
    w_qkv,
    q_gain,
    k_gain,
    w_out,
    ffn_norm,
    w_gate,
    w_up,
    w_down,
):
    f32, bf16 = jnp.float32, jnp.bfloat16
    rows, width = inputs.shape
    half_rows = rows // 2
    group_size = HQ // HK
    head_scale = HEAD ** (-0.5)
    seqs = lax.axis_size("z")
    ctx = lax.axis_index("x")
    member = 2 * lax.axis_index("y") + lax.axis_index("c")
    sequence = lax.axis_index("z")
    rank = MEMBERS * ctx + member

    where = jnp.stack([member, ctx]).astype(jnp.int32)
    norm_one = attn_norm.astype(f32)[:, None]
    norm_two = ffn_norm.astype(f32)[:, None]
    part_rows, ff = w_gate.shape
    qkv = w_qkv.shape[1]
    gain_width = q_gain.shape[0]
    out_rows = w_out.shape[0]
    half_width = width // 2
    gain_row = jnp.concatenate(
        [q_gain, k_gain, jnp.zeros((width - qkv - 2 * gain_width,), bf16)]
    )
    wide_qkv = jnp.concatenate(
        [
            (w_qkv * norm_one).astype(bf16),
            jnp.broadcast_to(gain_row[None], (part_rows, width - qkv)),
        ],
        axis=1,
    )
    attn_mine = lax.dynamic_slice_in_dim(
        jnp.concatenate([wide_qkv, w_out], axis=0), ctx * half_width, half_width, axis=1
    )
    attn_line = lax.all_gather(attn_mine, "z", axis=0)
    qkv_blocks = plane_gather(attn_line[:, :part_rows].reshape(-1, half_width))
    qkv_blocks = [block.reshape(seqs, part_rows, half_width) for block in qkv_blocks]
    weight_qkv = assemble(where, qkv_blocks).reshape(-1, width)
    gains = weight_qkv.reshape(-1, part_rows, width)[:, 0, qkv : qkv + 2 * gain_width]
    gain_query = gains[:, :gain_width].reshape(-1).astype(f32)
    gain_key = gains[:, gain_width:].reshape(-1).astype(f32)
    out_line = after(attn_line[:, part_rows:].reshape(-1, half_width), qkv_blocks[6])
    out_blocks = plane_gather(out_line)
    out_blocks = [block.reshape(seqs, out_rows, half_width) for block in out_blocks]
    aligned = out_rows % 16 == 0
    weight_out = (assemble if aligned else assemble_plain)(where, out_blocks)
    weight_out = weight_out.reshape(-1, width)

    piece = w_down.shape[0] // 2
    share = seqs * piece

    def chosen(weight):
        view = (weight * norm_two).astype(bf16).reshape(part_rows, seqs, MEMBERS, 2, piece)
        mine = lax.dynamic_index_in_dim(view, ctx, 3, keepdims=False)
        return mine.transpose(2, 0, 1, 3).reshape(MEMBERS, part_rows, share)

    weight_down = lax.all_gather(
        lax.dynamic_slice_in_dim(w_down, ctx * piece, piece), "z", axis=0, tiled=True
    )
    sent = lax.all_to_all(
        jnp.stack([chosen(w_gate), chosen(w_up)], axis=1),
        MEMBER,
        split_axis=0,
        concat_axis=0,
        tiled=True,
    )
    weight_gate = lax.all_gather(sent[:, 0].reshape(-1, share), "z", axis=0, tiled=True)
    weight_up = lax.all_gather(sent[:, 1].reshape(-1, share), "z", axis=0, tiled=True)

    slots = lax.dynamic_index_in_dim(block_index, sequence, 0, keepdims=False)
    segment_row = lax.dynamic_index_in_dim(segment_ids, sequence, 0, keepdims=False)
    valid_row = lax.dynamic_index_in_dim(pad_mask, sequence, 0, keepdims=False)
    index, bias = mask_tables(slots, segment_row, valid_row, rank, rows)
    own_blocks = lax.dynamic_slice_in_dim(slots, 2 * rank, 2)
    query_positions = (
        own_blocks[:, None] * half_rows + jnp.arange(half_rows, dtype=jnp.int32)[None, :]
    ).reshape(-1)
    angles = rope_angles(query_positions, HEAD)

    x_float = inputs.astype(f32)
    scale_one = inverse_rms(x_float)
    normed = (x_float * scale_one).astype(bf16)
    projected = jnp.dot(normed, weight_qkv, preferred_element_type=f32)
    query_raw = projected[:, : HQ * HEAD].reshape(rows, HQ, HEAD)
    key_raw = projected[:, HQ * HEAD : (HQ + HK) * HEAD].reshape(rows, HK, HEAD)
    value_part = projected[:, (HQ + HK) * HEAD : qkv].astype(bf16)
    query_scale = inverse_rms(query_raw)
    key_scale = inverse_rms(key_raw)
    key_part = rotate(key_raw * key_scale * gain_key, angles).astype(bf16)
    pairs = jnp.stack([key_part, value_part.reshape(rows, HK, HEAD)], axis=2)
    pair_blocks = plane_gather(pairs.reshape(rows, 2 * HK * HEAD))
    gathered = jnp.concatenate(pair_blocks, axis=0)
    queries = rotate(query_raw * query_scale * gain_query, angles).astype(bf16)
    queries = queries.reshape(rows, HQ * HEAD)
    mixed = attend(index, queries, gathered, bias)
    residual = x_float + jnp.dot(mixed, weight_out, preferred_element_type=f32)
    scale_two = inverse_rms(residual)
    normed_ffn = (residual * scale_two).astype(bf16)

    d_all = jnp.concatenate(plane_gather(after(cotangent, pair_blocks[6])), axis=0)
    n_all = jnp.concatenate(plane_gather(normed_ffn), axis=0)
    d_hidden = jnp.einsum("td,fd->tf", d_all, weight_down, preferred_element_type=f32)
    gate_pre = jnp.dot(n_all, weight_gate, preferred_element_type=f32)
    up_pre = jnp.dot(n_all, weight_up, preferred_element_type=f32)
    gate_sigmoid = jax.nn.sigmoid(gate_pre)
    hidden = (gate_pre * gate_sigmoid * up_pre).astype(bf16)
    d_gate = (d_hidden * up_pre * gate_sigmoid * (1.0 + gate_pre * (1.0 - gate_sigmoid))).astype(
        bf16
    )
    d_up = (d_hidden * gate_pre * gate_sigmoid).astype(bf16)
    d_normed_terms = jnp.einsum(
        "tf,df->td", d_gate, weight_gate, preferred_element_type=f32
    ) + jnp.einsum("tf,df->td", d_up, weight_up, preferred_element_type=f32)
    d_normed_ffn = plane_scatter(d_normed_terms.reshape(2 * MEMBERS, rows, width))
    late_hidden = after(hidden, d_normed_ffn)
    output_terms = jnp.dot(late_hidden, weight_down, preferred_element_type=f32)
    output = (residual + plane_scatter(output_terms.reshape(2 * MEMBERS, rows, width))).astype(
        bf16
    )
    down_term = jnp.einsum("tf,td->fd", hidden, d_all, preferred_element_type=f32)
    gate_term = jnp.einsum("td,tf->df", n_all, d_gate, preferred_element_type=f32)
    up_term = jnp.einsum("td,tf->df", n_all, d_up, preferred_element_type=f32)

    def z_sum(term):
        return lax.psum_scatter(term.astype(bf16), "z", scatter_dimension=0, tiled=True)

    down_sum = z_sum(down_term)
    gate_sum = z_sum(gate_term)
    up_sum = z_sum(up_term)

    d_residual = cotangent.astype(f32) + norm_back(d_normed_ffn, residual, scale_two)
    d_attn = d_residual.astype(bf16)
    out_term = jnp.einsum("tc,td->cd", mixed, d_attn, preferred_element_type=f32)
    d_mixed = jnp.einsum("td,cd->tc", d_attn, weight_out, preferred_element_type=f32).astype(bf16)
    d_query, kv_terms = attend_back(
        index, queries, gathered, d_mixed, bias.transpose(0, 2, 1)
    )
    d_query = d_query.reshape(rows, HQ, HEAD)
    d_pairs = plane_scatter(kv_terms.reshape(2 * MEMBERS, rows, 2 * HK * HEAD))
    d_pairs = d_pairs.reshape(rows, HK, 2, HEAD)
    d_key = d_pairs[:, :, 0]
    d_value = d_pairs[:, :, 1].reshape(rows, HK * HEAD)
    d_query_normed = rotate_back(d_query, angles)
    d_key_normed = rotate_back(d_key, angles)
    q_gain_term = jnp.sum(d_query_normed * query_raw * query_scale, axis=(0, 1))
    k_gain_term = jnp.sum(d_key_normed * key_raw * key_scale, axis=(0, 1))
    d_query_raw = norm_back(d_query_normed * gain_query, query_raw, query_scale)
    d_key_raw = norm_back(d_key_normed * gain_key, key_raw, key_scale)
    d_projected = jnp.concatenate(
        [
            d_query_raw.reshape(rows, HQ * HEAD),
            d_key_raw.reshape(rows, HK * HEAD),
            d_value,
            jnp.zeros((rows, width - qkv), f32),
        ],
        axis=1,
    ).astype(bf16)
    qkv_term = jnp.einsum("td,tc->dc", normed, d_projected, preferred_element_type=f32)
    d_normed = jnp.einsum("tc,dc->td", d_projected, weight_qkv, preferred_element_type=f32)
    input_grad = (d_residual + norm_back(d_normed, x_float, scale_one)).astype(bf16)

    def both(mine):
        other = swapped(mine, "x")
        low = jnp.where(ctx == 0, mine, other)
        high = jnp.where(ctx == 0, other, mine)
        return low, high

    def summed(terms):
        seqs_, rows_, half_ = terms.shape[1:]
        mine = plane_scatter(terms.reshape(2 * MEMBERS, seqs_ * rows_, half_)).astype(bf16)
        mine = lax.psum_scatter(mine, "z", scatter_dimension=0, tiled=True)
        return jnp.concatenate(both(mine), axis=1).astype(f32)

    def placed(total):
        moved = lax.all_to_all(
            total.reshape(MEMBERS, part_rows, share),
            MEMBER,
            split_axis=0,
            concat_axis=0,
            tiled=True,
        )
        low, high = both(moved)
        whole = jnp.stack([low, high]).reshape(2, MEMBERS, part_rows, seqs, piece)
        return whole.transpose(2, 3, 1, 0, 4).reshape(part_rows, ff).astype(f32)

    gate_raw = placed(gate_sum)
    up_raw = placed(up_sum)
    ffn_norm_grad = jnp.sum(
        gate_raw * w_gate.astype(f32) + up_raw * w_up.astype(f32), axis=1
    )
    down_grad = jnp.concatenate(both(down_sum), axis=0).astype(f32)
    out_whole = out_term.astype(bf16).reshape(seqs, MEMBERS, out_rows, width)
    out_grad = summed((split if aligned else split_plain)(where, out_whole))
    gain_terms = jnp.stack([q_gain_term, k_gain_term]).reshape(2, -1, gain_width)
    gain_terms = gain_terms.transpose(1, 0, 2).reshape(seqs, MEMBERS, 1, 2 * gain_width)
    gain_terms = jnp.pad(gain_terms, ((0, 0), (0, 0), (0, 0), (0, LANES - 2 * gain_width)))
    qkv_whole = qkv_term.astype(bf16).reshape(seqs, MEMBERS, part_rows, width)
    qkv_all = summed(split(where, qkv_whole, gain_terms))
    qkv_raw = qkv_all[:, :qkv]
    gain_grads = qkv_all[0, qkv:]
    attn_norm_grad = jnp.sum(qkv_raw * w_qkv.astype(f32), axis=1)
    return (
        output,
        input_grad,
        attn_norm_grad,
        qkv_raw * norm_one,
        gain_grads[:gain_width],
        gain_grads[gain_width : 2 * gain_width],
        out_grad,
        ffn_norm_grad,
        gate_raw * norm_two,
        up_raw * norm_two,
        down_grad,
    )


def solution(mesh):
    fsdp = mesh.shape["fsdp"]
    devices = mesh.devices.reshape(2, fsdp // MEMBERS, 2, 2)
    inner = jax.sharding.Mesh(devices, ("x", "z", "y", "c"))
    tokens = P(("x",) + FSDP, None)
    return jax.shard_map(
        shards,
        mesh=inner,
        in_specs=(
            tokens,
            tokens,
            P(),
            P(),
            P(),
            P(FSDP),
            P(FSDP, None),
            P(FSDP),
            P(FSDP),
            P(FSDP, None),
            P(FSDP),
            P(FSDP, None),
            P(FSDP, None),
            P(FSDP, None),
        ),
        out_specs=(
            tokens,
            tokens,
            P(FSDP),
            P(FSDP, None),
            P(FSDP),
            P(FSDP),
            P(FSDP, None),
            P(FSDP),
            P(FSDP, None),
            P(FSDP, None),
            P(FSDP, None),
        ),
        check_vma=False,
    )
```

```python
import functools

import jax
import jax.numpy as jnp
from jax import lax
from jax.experimental import pallas as pl
from jax.experimental.pallas import tpu as pltpu
from jax.sharding import PartitionSpec as P

HQ = 20
HK = 5
HEAD = 64
WINDOW = 1024
MEMBERS = 4


EPSILON = 1e-06
MASKED = -1e30
LANES = 128
ROPE_BASE = 10000.0


SEQUENCE = ("x", "y", "c")
MEMBER = ("y", "c")
FSDP = ("z", "y", "c")


def swapped(array, axis):
    return lax.ppermute(array, axis, [(0, 1), (1, 0)])


def plane_gather(block):
    half = block.shape[0] // 2
    by_x = swapped(block, "x")
    by_y = swapped(block, "y")
    by_c = swapped(block, "c")
    far = jnp.concatenate([swapped(by_x[:half], "y"), swapped(by_y[half:], "x")], axis=0)
    return [
        block,
        by_c,
        by_y,
        swapped(by_y, "c"),
        by_x,
        swapped(by_x, "c"),
        far,
        swapped(far, "c"),
    ]


def added(one, other):
    return one.astype(jnp.float32) + other.astype(jnp.float32)


def plane_scatter(keep, send):
    chip = [
        added(keep[p], swapped(send[p], "c")).astype(jnp.bfloat16) for p in range(MEMBERS)
    ]
    return chip_scatter(chip)


def chip_scatter(chip):
    half = chip[0].shape[0] // 2
    first = [part[:half] for part in chip]
    second = [part[half:] for part in chip]
    far_x, far_y = swapped(first[3], "x"), swapped(second[3], "y")
    near_x, near_y = swapped(first[2], "x"), swapped(second[1], "y")
    last_y = swapped(added(first[1], far_x).astype(jnp.bfloat16), "y")
    last_x = swapped(added(second[2], far_y).astype(jnp.bfloat16), "x")
    return jnp.concatenate(
        [
            added(first[0], near_x) + last_y.astype(jnp.float32),
            added(second[0], near_y) + last_x.astype(jnp.float32),
        ],
        axis=0,
    )


def plane_scatter_stacked(keep, send):
    chip = added(keep, swapped(send, "c")).astype(jnp.bfloat16)
    return chip_scatter([chip[p] for p in range(MEMBERS)])


def inverse_rms(values):
    return lax.rsqrt(jnp.mean(values * values, axis=-1, keepdims=True) + EPSILON)


def rope_angles(positions, width):
    frequencies = ROPE_BASE ** (-2.0 * jnp.arange(width // 2, dtype=jnp.float32) / width)
    return positions.astype(jnp.float32)[:, None] * frequencies[None, :]


def rotate(values, angles):
    cosine_table = jnp.cos(angles)[:, None, :]
    sine_table = jnp.sin(angles)[:, None, :]
    half_width = values.shape[-1] // 2
    first_half = values[..., :half_width]
    second_half = values[..., half_width:]
    return jnp.concatenate(
        [
            first_half * cosine_table - second_half * sine_table,
            second_half * cosine_table + first_half * sine_table,
        ],
        axis=-1,
    )


def rotate_back(values, angles):
    cosine_table = jnp.cos(angles)[:, None, :]
    sine_table = jnp.sin(angles)[:, None, :]
    half_width = values.shape[-1] // 2
    first_half = values[..., :half_width]
    second_half = values[..., half_width:]
    return jnp.concatenate(
        [
            first_half * cosine_table + second_half * sine_table,
            second_half * cosine_table - first_half * sine_table,
        ],
        axis=-1,
    )


def norm_back(incoming, values, scale_inv):
    return scale_inv * (
        incoming
        - values * scale_inv * scale_inv * jnp.mean(incoming * values, axis=-1, keepdims=True)
    )


def taken(index_ref, half, slots, block, kv_ref):
    parts = []
    for slot in range(slots):
        start = pl.multiple_of(index_ref[half * slots + slot] * block, block)
        parts.append(kv_ref[pl.ds(start, block), :])
    return jnp.concatenate(parts, axis=0)


def grouped(ref, half, block, group):
    wide = ref[pl.ds(half * block, block), :]
    return jnp.concatenate(
        [wide[:, g * HEAD : (g + 1) * HEAD] for g in range(group)], axis=0
    )


def attend_kernel(slots, block, group, index_ref, q_ref, kv_ref, bias_ref, mixed_ref):
    rows = group * block
    for half in range(2):
        pair = taken(index_ref, half, slots, block, kv_ref)
        keys = pair[:, :HEAD]
        lane = lax.broadcasted_iota(jnp.int32, pair.shape, 1)
        values = jnp.where(lane < HEAD, jnp.ones_like(pair), pair)
        query = grouped(q_ref, half, block, group) * jnp.bfloat16(HEAD ** (-0.5))
        scores = lax.dot_general(
            query, keys, (((1,), (1,)), ((), ())), preferred_element_type=jnp.float32
        )
        bias = bias_ref[half]
        weights = jnp.exp(scores + jnp.concatenate([bias] * group, axis=0)).astype(jnp.bfloat16)
        total = jnp.dot(weights, values, preferred_element_type=jnp.float32)
        result = (total[:, HEAD:] / total[:, :HEAD]).astype(jnp.bfloat16)
        for g in range(group):
            mixed_ref[half * block : (half + 1) * block, g * HEAD : (g + 1) * HEAD] = result[
                g * block : (g + 1) * block
            ]


def attend(index, queries, pairs, bias):
    rows = queries.shape[0]
    block = rows // 2
    slots = WINDOW // block + 1
    group = HQ // HK
    wide = group * HEAD
    return pl.pallas_call(
        functools.partial(attend_kernel, slots, block, group),
        grid_spec=pltpu.PrefetchScalarGridSpec(
            num_scalar_prefetch=1,
            grid=(HK,),
            in_specs=[
                pl.BlockSpec((rows, wide), lambda h, index: (0, h)),
                pl.BlockSpec((pairs.shape[0], 2 * HEAD), lambda h, index: (0, h)),
                pl.BlockSpec(bias.shape, lambda h, index: (0, 0, 0)),
            ],
            out_specs=pl.BlockSpec((rows, wide), lambda h, index: (0, h)),
        ),
        out_shape=jax.ShapeDtypeStruct(queries.shape, jnp.bfloat16),
        name="attend",
    )(index, queries, pairs, bias)


def attend_back_kernel(
    slots, block, group, index_ref, q_ref, kv_ref, dm_ref, bias_ref, dq_ref, dkv_ref, sums
):
    scale = jnp.bfloat16(HEAD ** (-0.5))
    sums[...] = jnp.zeros_like(sums)
    nt = (((1,), (1,)), ((), ()))
    for half in range(2):
        pair = taken(index_ref, half, slots, block, kv_ref)
        keys = pair[:, :HEAD]
        values = pair[:, HEAD:]
        query = grouped(q_ref, half, block, group) * scale
        grads = grouped(dm_ref, half, block, group)
        scores = lax.dot_general(keys, query, nt, preferred_element_type=jnp.float32)
        bias = bias_ref[half]
        weights = jnp.exp(scores + jnp.concatenate([bias] * group, axis=1))
        probs = weights * (1.0 / jnp.sum(weights, axis=0, keepdims=True))
        d_probs = lax.dot_general(values, grads, nt, preferred_element_type=jnp.float32)
        delta = jnp.sum(probs * d_probs, axis=0, keepdims=True)
        d_scores = (probs * (d_probs - delta)).astype(jnp.bfloat16)
        d_values = jnp.dot(probs.astype(jnp.bfloat16), grads, preferred_element_type=jnp.float32)
        d_keys = jnp.dot(d_scores, query, preferred_element_type=jnp.float32)
        both = jnp.concatenate([d_keys, d_values], axis=1)
        for slot in range(slots):
            start = pl.multiple_of(index_ref[half * slots + slot] * block, block)
            sums[pl.ds(start, block), :] += both[slot * block : (slot + 1) * block]
        d_query = jnp.dot(
            (keys * scale).T, d_scores, preferred_element_type=jnp.float32
        )
        for g in range(group):
            dq_ref[half * block : (half + 1) * block, g * HEAD : (g + 1) * HEAD] = d_query[
                :, g * block : (g + 1) * block
            ].T
    dkv_ref[...] = sums[...].astype(jnp.bfloat16)


def attend_back(index, queries, pairs, d_mixed, bias):
    rows = queries.shape[0]
    block = rows // 2
    slots = WINDOW // block + 1
    group = HQ // HK
    wide = group * HEAD
    keys = pairs.shape[0]
    return pl.pallas_call(
        functools.partial(attend_back_kernel, slots, block, group),
        grid_spec=pltpu.PrefetchScalarGridSpec(
            num_scalar_prefetch=1,
            grid=(HK,),
            in_specs=[
                pl.BlockSpec((rows, wide), lambda h, index: (0, h)),
                pl.BlockSpec((keys, 2 * HEAD), lambda h, index: (0, h)),
                pl.BlockSpec((rows, wide), lambda h, index: (0, h)),
                pl.BlockSpec(bias.shape, lambda h, index: (0, 0, 0)),
            ],
            out_specs=[
                pl.BlockSpec((rows, wide), lambda h, index: (0, h)),
                pl.BlockSpec((keys, 2 * HEAD), lambda h, index: (0, h)),
            ],
            scratch_shapes=[pltpu.VMEM((keys, 2 * HEAD), jnp.float32)],
        ),
        out_shape=[
            jax.ShapeDtypeStruct(queries.shape, jnp.float32),
            jax.ShapeDtypeStruct(pairs.shape, jnp.bfloat16),
        ],
        name="attend_back",
    )(index, queries, pairs, d_mixed, bias)


def mask_tables(block_index_row, segment_row, valid_row, rank, rows):
    block = rows // 2
    slots = WINDOW // block + 1
    blocks = block_index_row.shape[0]
    own = lax.dynamic_slice_in_dim(block_index_row, 2 * rank, 2)
    wanted = own[:, None] - jnp.arange(slots, dtype=jnp.int32)[None, :]
    there = wanted >= 0
    wanted = jnp.maximum(wanted, 0)
    match = wanted[:, :, None] == block_index_row[None, None, :]
    place = jnp.sum(
        jnp.where(match, jnp.arange(blocks, dtype=jnp.int32)[None, None, :], 0), axis=-1
    )
    index = 2 * jnp.bitwise_xor(place // 2, rank) + place % 2
    segments = segment_row.reshape(blocks, block)
    valid = valid_row.reshape(blocks, block)

    def rows_of(table, at):
        hot = (at[..., None] == jnp.arange(blocks, dtype=jnp.int32)).astype(jnp.float32)
        return jnp.einsum("...b,bj->...j", hot, table.astype(jnp.float32), precision=lax.Precision.HIGHEST)

    own_segments = rows_of(segments, own)
    key_segments = rows_of(segments, wanted)
    key_valid = rows_of(valid, wanted)
    offset = (
        jnp.arange(block, dtype=jnp.int32)[:, None, None]
        - jnp.arange(block, dtype=jnp.int32)[None, None, :]
        + block * jnp.arange(slots, dtype=jnp.int32)[None, :, None]
    )
    allowed = (
        ((offset >= 0) & (offset < WINDOW))[None]
        & there[:, None, :, None]
        & (own_segments[:, :, None, None] == key_segments[:, None])
        & ((key_valid[:, None] == 1.0) | (offset == 0)[None])
    )
    bias = jnp.where(allowed, 0.0, -1e30).astype(jnp.float32).reshape(2, block, slots * block)
    return index.reshape(-1).astype(jnp.int32), bias


def zero_of(*values):
    firsts = [value[(0,) * value.ndim].astype(jnp.float32) for value in values]
    return sum(firsts) * 0.0


def full(array):
    return pl.BlockSpec(array.shape, lambda *_: (0,) * array.ndim)


def ffn_up_kernel(count, *refs):
    blocks, (gate_w, up_w) = refs[:count], refs[count : count + 2]
    hidden_ref, gate_ref, up_ref = refs[count + 2 :]
    rows = blocks[0].shape[0]
    weight = jnp.concatenate([gate_w[...], up_w[...]], axis=1)
    for pair in range(count // 2):
        tokens = jnp.concatenate([blocks[2 * pair][...], blocks[2 * pair + 1][...]], axis=0)
        both = jnp.dot(tokens, weight, preferred_element_type=jnp.float32)
        gate, up = both[:, :LANES], both[:, LANES:]
        sigmoid = 1.0 / (1.0 + jnp.exp(-gate))
        silu = gate * sigmoid
        at = slice(2 * pair * rows, 2 * (pair + 1) * rows)
        hidden_ref[at, :] = (silu * up).astype(jnp.bfloat16)
        gate_ref[at, :] = (up * sigmoid * (1.0 + gate * (1.0 - sigmoid))).astype(jnp.bfloat16)
        up_ref[at, :] = silu.astype(jnp.bfloat16)


def ffn_up(blocks, weight):
    rows, width = blocks[0].shape
    share = weight.shape[1] // 2
    count = len(blocks)
    tiles = share // LANES
    out = jax.ShapeDtypeStruct((count * rows, share), jnp.bfloat16)
    spec = pl.BlockSpec((count * rows, LANES), lambda i: (0, i))
    return pl.pallas_call(
        functools.partial(ffn_up_kernel, count),
        grid=(tiles,),
        in_specs=[full(block) for block in blocks]
        + [
            pl.BlockSpec((width, LANES), lambda i: (0, i)),
            pl.BlockSpec((width, LANES), lambda i: (0, tiles + i)),
        ],
        out_specs=[spec] * 3,
        out_shape=[out] * 3,
        cost_estimate=pl.CostEstimate(
            flops=4 * count * rows * width * share,
            transcendentals=count * rows * share,
            bytes_accessed=2 * count * rows * width,
        ),
        name="ffn_up",
    )(*blocks, weight, weight)


def ffn_back_kernel(count, *refs):
    grads, rest = refs[:count], refs[count:]
    _, gate_ref, up_ref, down_ref, weight_ref, d_ref, *outs = rest
    rows = grads[0].shape[0]
    nt = (((1,), (1,)), ((), ()))
    for pair in range(count // 2):
        at = slice(2 * pair * rows, 2 * (pair + 1) * rows)
        d_out = jnp.concatenate([grads[2 * pair][...], grads[2 * pair + 1][...]], axis=0)
        d_hidden = lax.dot_general(
            d_out, down_ref[...], nt, preferred_element_type=jnp.float32
        )
        d_gate = (d_hidden * gate_ref[at, :].astype(jnp.float32)).astype(jnp.bfloat16)
        d_up = (d_hidden * up_ref[at, :].astype(jnp.float32)).astype(jnp.bfloat16)
        d_both = jnp.concatenate([d_gate, d_up], axis=1)
        d_ref[at, :] = d_both
        d_in = lax.dot_general(
            d_both, weight_ref[...], nt, preferred_element_type=jnp.float32
        ).astype(jnp.bfloat16)
        outs[2 * pair][...] = d_in[:rows]
        outs[2 * pair + 1][...] = d_in[rows:]


def ffn_back(token, grads, gate, up, place, down, weight):
    count = len(grads)
    rows, width = grads[0].shape
    share = down.shape[0]
    factors = pl.BlockSpec((count * rows, share), lambda i: (place, 0))
    block = jax.ShapeDtypeStruct((rows, width), jnp.bfloat16)
    d_both = jax.ShapeDtypeStruct((count * rows, 2 * share), jnp.bfloat16)
    d_both, *terms = pl.pallas_call(
        functools.partial(ffn_back_kernel, count),
        grid=(1,),
        in_specs=[full(grad) for grad in grads]
        + [pl.BlockSpec(memory_space=pltpu.SMEM), factors, factors, full(down), full(weight)],
        out_specs=[full(d_both)] + [full(block)] * count,
        out_shape=[d_both] + [block] * count,
        cost_estimate=pl.CostEstimate(
            flops=6 * count * rows * width * share,
            transcendentals=0,
            bytes_accessed=4 * count * rows * width,
        ),
        name="ffn_back",
    )(*grads, token, gate, up, down, weight)
    return d_both, terms


def ffn_out_kernel(token_ref, hidden_ref, down_ref, *outs):
    rows = outs[0].shape[0]
    for pair in range(len(outs) // 2):
        at = slice(2 * pair * rows, 2 * (pair + 1) * rows)
        term = jnp.dot(
            hidden_ref[at, :], down_ref[...], preferred_element_type=jnp.float32
        ).astype(jnp.bfloat16)
        outs[2 * pair][...] = term[:rows]
        outs[2 * pair + 1][...] = term[rows:]


def ffn_out(token, hidden, down, count):
    share, width = down.shape
    rows = hidden.shape[0] // count
    tile = width // 4
    block = jax.ShapeDtypeStruct((rows, width), jnp.bfloat16)
    return pl.pallas_call(
        ffn_out_kernel,
        grid=(4,),
        in_specs=[
            pl.BlockSpec(memory_space=pltpu.SMEM),
            full(hidden),
            pl.BlockSpec((share, tile), lambda i: (0, i)),
        ],
        out_specs=[pl.BlockSpec((rows, tile), lambda i: (0, i))] * count,
        out_shape=[block] * count,
        cost_estimate=pl.CostEstimate(
            flops=2 * count * rows * width * share,
            transcendentals=0,
            bytes_accessed=2 * count * rows * width,
        ),
        name="ffn_out",
    )(token, hidden, down)


def summed_products(lefts, rights, out_ref):
    total = None
    for left, right in zip(lefts, rights):
        term = lax.dot_general(
            left, right, (((0,), (0,)), ((), ())), preferred_element_type=jnp.float32
        )
        total = term if total is None else total + term
    out_ref[...] = total.astype(jnp.bfloat16)


def in_grad_kernel(count, *refs):
    blocks, grads, out_ref = refs[:count], refs[count:-1], refs[-1]
    rows = blocks[0].shape[0]
    pieces = []
    for grad in grads:
        pieces += [grad[k * rows : (k + 1) * rows, :] for k in range(grad.shape[0] // rows)]
    summed_products([block[...] for block in blocks], pieces, out_ref)


def in_grad(blocks, grads, tile):
    rows, width = blocks[0].shape
    columns = grads[0].shape[1]
    count = len(blocks)
    return pl.pallas_call(
        functools.partial(in_grad_kernel, count),
        grid=(width // tile,),
        in_specs=[pl.BlockSpec((rows, tile), lambda i: (0, i))] * count
        + [full(grad) for grad in grads],
        out_specs=pl.BlockSpec((tile, columns), lambda i: (i, 0)),
        out_shape=jax.ShapeDtypeStruct((width, columns), jnp.bfloat16),
        cost_estimate=pl.CostEstimate(
            flops=2 * count * rows * width * columns,
            transcendentals=0,
            bytes_accessed=2 * count * rows * (width + columns),
        ),
        name="in_grad",
    )(*blocks, *grads)


def down_grad_kernel(hidden_ref, *refs):
    *blocks, out_ref = refs
    rows = blocks[0].shape[0]
    lefts = [hidden_ref[k * rows : (k + 1) * rows, :] for k in range(len(blocks))]
    summed_products(lefts, [block[...] for block in blocks], out_ref)


def down_gradient(hidden, blocks, tile):
    rows, width = blocks[0].shape
    share = hidden.shape[1]
    count = len(blocks)
    return pl.pallas_call(
        down_grad_kernel,
        grid=(width // tile,),
        in_specs=[full(hidden)] + [pl.BlockSpec((rows, tile), lambda i: (0, i))] * count,
        out_specs=pl.BlockSpec((share, tile), lambda i: (0, i)),
        out_shape=jax.ShapeDtypeStruct((share, width), jnp.bfloat16),
        cost_estimate=pl.CostEstimate(
            flops=2 * count * rows * width * share,
            transcendentals=0,
            bytes_accessed=2 * count * rows * (width + share),
        ),
        name="down_gradient",
    )(hidden, *blocks)


def assemble_kernel(where_ref, *refs):
    *blocks, whole = refs
    half = whole.shape[3] // 2
    for k, block in enumerate(blocks):
        member = jnp.bitwise_xor(where_ref[0], k % MEMBERS)
        start = pl.multiple_of(jnp.bitwise_xor(where_ref[1], k // MEMBERS) * half, LANES)
        whole[:, pl.ds(member, 1), :, pl.ds(start, half)] = block[...][:, None]


def assemble(where, blocks):
    seqs, rows, half = blocks[0].shape
    return pl.pallas_call(
        assemble_kernel,
        in_specs=[pl.BlockSpec(memory_space=pltpu.SMEM)]
        + [pl.BlockSpec(memory_space=pltpu.VMEM)] * len(blocks),
        out_specs=pl.BlockSpec(memory_space=pltpu.VMEM),
        out_shape=jax.ShapeDtypeStruct((seqs, MEMBERS, rows, 2 * half), blocks[0].dtype),
        name="assemble",
    )(where, *blocks)


def terms_kernel(where_ref, left_ref, right_ref, *refs):
    *extra, keep_ref, send_ref, turned = refs
    k = pl.program_id(0)
    seqs, rows, half = keep_ref.shape[1:]

    @pl.when(k == 0)
    def _():
        turned[...] = left_ref[...].T

    member = jnp.bitwise_xor(where_ref[0], k % MEMBERS)
    parts = []
    for z in range(seqs):
        start = pl.multiple_of((z * MEMBERS + member) * rows, 16)
        parts.append(turned[pl.ds(start, rows), :])
    term = jnp.dot(
        jnp.concatenate(parts, axis=0), right_ref[...], preferred_element_type=jnp.float32
    ).astype(jnp.bfloat16)
    term = term.reshape(1, seqs, rows, half)

    def store(ref):
        ref[...] = term
        if extra:

            @pl.when(jnp.bitwise_xor(where_ref[1], k // MEMBERS) == 1)
            def _():
                shape = (1, seqs, rows, LANES)
                ref[..., half - LANES :] = jnp.broadcast_to(extra[0][:, 0][None], shape).astype(
                    jnp.bfloat16
                )

    pl.when(k % 2 == 0)(lambda: store(keep_ref))
    pl.when(k % 2 == 1)(lambda: store(send_ref))


def gradient_terms(where, left, right, extra=None):
    seqs = lax.axis_size("z")
    tokens, height = left.shape
    rows = height // (seqs * MEMBERS)
    half = right.shape[1] // 2
    if rows % 16:
        whole = jnp.einsum("tr,tc->rc", left, right, preferred_element_type=jnp.float32)
        whole = whole.astype(jnp.bfloat16).reshape(seqs, MEMBERS, rows, 2 * half)
        terms = split_plain(where, whole)
        return terms[::2], terms[1::2]
    in_specs = [
        pl.BlockSpec((tokens, height), lambda k, where: (0, 0)),
        pl.BlockSpec(
            (tokens, half), lambda k, where: (0, jnp.bitwise_xor(where[1], k // MEMBERS))
        ),
    ]
    operands = [left, right]
    if extra is not None:
        in_specs.append(
            pl.BlockSpec(
                (seqs, 1, 1, LANES),
                lambda k, where: (0, jnp.bitwise_xor(where[0], k % MEMBERS), 0, 0),
            )
        )
        operands.append(extra)
    spec = pl.BlockSpec((1, seqs, rows, half), lambda k, where: (k // 2, 0, 0, 0))
    shape = jax.ShapeDtypeStruct((MEMBERS, seqs, rows, half), jnp.bfloat16)
    return pl.pallas_call(
        terms_kernel,
        grid_spec=pltpu.PrefetchScalarGridSpec(
            num_scalar_prefetch=1,
            grid=(2 * MEMBERS,),
            in_specs=in_specs,
            out_specs=[spec, spec],
            scratch_shapes=[pltpu.VMEM((height, tokens), jnp.bfloat16)],
        ),
        out_shape=[shape, shape],
        name="gradient_terms",
    )(where, *operands)


def assemble_plain(where, blocks):
    order = jnp.bitwise_xor(MEMBERS * where[1] + where[0], jnp.arange(2 * MEMBERS))
    seqs, rows, half = blocks[0].shape
    kept = jnp.take(jnp.stack(blocks), order, axis=0)
    kept = kept.reshape(2, MEMBERS, seqs, rows, half)
    return kept.transpose(2, 1, 3, 0, 4).reshape(seqs, MEMBERS, rows, 2 * half)


def split_plain(where, whole):
    order = jnp.bitwise_xor(MEMBERS * where[1] + where[0], jnp.arange(2 * MEMBERS))
    seqs, members, rows, columns = whole.shape
    parts = whole.reshape(seqs, members, rows, 2, columns // 2).transpose(3, 1, 0, 2, 4)
    return jnp.take(parts.reshape(2 * members, seqs, rows, columns // 2), order, axis=0)


def shards(
    inputs,
    cotangent,
    segment_ids,
    pad_mask,
    block_index,
    attn_norm,
    w_qkv,
    q_gain,
    k_gain,
    w_out,
    ffn_norm,
    w_gate,
    w_up,
    w_down,
):
    f32, bf16 = jnp.float32, jnp.bfloat16
    rows, width = inputs.shape
    half_rows = rows // 2
    group_size = HQ // HK
    head_scale = HEAD ** (-0.5)
    seqs = lax.axis_size("z")
    ctx = lax.axis_index("x")
    member = 2 * lax.axis_index("y") + lax.axis_index("c")
    sequence = lax.axis_index("z")
    rank = MEMBERS * ctx + member

    where = jnp.stack([member, ctx]).astype(jnp.int32)
    norm_one = attn_norm.astype(f32)[:, None]
    norm_two = ffn_norm.astype(f32)[:, None]
    part_rows, ff = w_gate.shape
    qkv = w_qkv.shape[1]
    gain_width = q_gain.shape[0]
    out_rows = w_out.shape[0]
    half_width = width // 2
    gain_row = jnp.concatenate(
        [q_gain, k_gain, jnp.zeros((width - qkv - 2 * gain_width,), bf16)]
    )
    wide_qkv = jnp.concatenate(
        [
            (w_qkv * norm_one).astype(bf16),
            jnp.broadcast_to(gain_row[None], (part_rows, width - qkv)),
        ],
        axis=1,
    )
    attn_mine = lax.dynamic_slice_in_dim(
        jnp.concatenate([wide_qkv, w_out], axis=0), ctx * half_width, half_width, axis=1
    )
    attn_line = lax.all_gather(attn_mine, "z", axis=0)
    qkv_blocks = plane_gather(attn_line[:, :part_rows].reshape(-1, half_width))
    qkv_blocks = [block.reshape(seqs, part_rows, half_width) for block in qkv_blocks]
    weight_qkv = assemble(where, qkv_blocks).reshape(-1, width)
    gains = weight_qkv.reshape(-1, part_rows, width)[:, 0, qkv : qkv + 2 * gain_width]
    gain_query = gains[:, :gain_width].reshape(-1).astype(f32)
    gain_key = gains[:, gain_width:].reshape(-1).astype(f32)
    out_line = attn_line[:, part_rows:].reshape(-1, half_width)
    out_line = out_line + zero_of(qkv_blocks[6]).astype(bf16)
    out_blocks = plane_gather(out_line)
    out_blocks = [block.reshape(seqs, out_rows, half_width) for block in out_blocks]
    aligned = out_rows % 16 == 0
    weight_out = (assemble if aligned else assemble_plain)(where, out_blocks)
    weight_out = weight_out.reshape(-1, width)

    piece = w_down.shape[0] // 2
    share = seqs * piece

    def chosen(weight):
        view = (weight * norm_two).astype(bf16).reshape(part_rows, seqs, MEMBERS, 2, piece)
        mine = lax.dynamic_index_in_dim(view, ctx, 3, keepdims=False)
        return mine.transpose(2, 0, 1, 3).reshape(MEMBERS, part_rows, share)

    sent = lax.all_to_all(
        jnp.concatenate([chosen(w_gate), chosen(w_up)], axis=2),
        MEMBER,
        split_axis=0,
        concat_axis=0,
        tiled=True,
    )
    weight_in = lax.all_gather(sent.reshape(-1, 2 * share), "z", axis=0, tiled=True)
    down_mine = lax.dynamic_slice_in_dim(w_down, ctx * piece, piece)
    weight_down = lax.all_gather(
        down_mine + zero_of(sent).astype(bf16), "z", axis=0, tiled=True
    )

    slots = lax.dynamic_index_in_dim(block_index, sequence, 0, keepdims=False)
    segment_row = lax.dynamic_index_in_dim(segment_ids, sequence, 0, keepdims=False)
    valid_row = lax.dynamic_index_in_dim(pad_mask, sequence, 0, keepdims=False)
    index, bias = mask_tables(slots, segment_row, valid_row, rank, rows)
    own_blocks = lax.dynamic_slice_in_dim(slots, 2 * rank, 2)
    query_positions = (
        own_blocks[:, None] * half_rows + jnp.arange(half_rows, dtype=jnp.int32)[None, :]
    ).reshape(-1)
    angles = rope_angles(query_positions, HEAD)

    x_float = inputs.astype(f32)
    scale_one = inverse_rms(x_float)
    normed = (x_float * scale_one).astype(bf16)
    projected = jnp.dot(normed, weight_qkv, preferred_element_type=f32)
    query_raw = projected[:, : HQ * HEAD].reshape(rows, HQ, HEAD)
    key_raw = projected[:, HQ * HEAD : (HQ + HK) * HEAD].reshape(rows, HK, HEAD)
    value_part = projected[:, (HQ + HK) * HEAD : qkv].astype(bf16)
    query_scale = inverse_rms(query_raw)
    key_scale = inverse_rms(key_raw)
    key_part = rotate(key_raw * key_scale * gain_key, angles).astype(bf16)
    pairs = jnp.stack([key_part, value_part.reshape(rows, HK, HEAD)], axis=2)
    pair_blocks = plane_gather(pairs.reshape(rows, 2 * HK * HEAD))
    gathered = jnp.concatenate(pair_blocks, axis=0)
    queries = rotate(query_raw * query_scale * gain_query, angles).astype(bf16)
    queries = queries.reshape(rows, HQ * HEAD)
    mixed = attend(index, queries, gathered, bias)
    residual = x_float + jnp.dot(mixed, weight_out, preferred_element_type=f32)
    scale_two = inverse_rms(residual)
    normed_ffn = (residual * scale_two).astype(bf16)

    late_cotangent = cotangent + zero_of(pair_blocks[6]).astype(bf16)
    d_blocks = plane_gather(late_cotangent)
    d_blocks[0] = cotangent
    n_blocks = plane_gather(normed_ffn)
    hidden, gate_factor, up_factor = ffn_up(n_blocks, weight_in)
    tile = width // 4
    down_term = down_gradient(hidden, d_blocks, tile)
    token = zero_of(down_term).reshape(1)
    order = ((3,), (1, 2), (0,))
    d_both = {}
    keep, send = [None] * MEMBERS, [None] * MEMBERS
    for part in order:
        grads = [d_blocks[2 * p + s] for p in part for s in range(2)]
        factors = (gate_factor, up_factor)
        place = part[0]
        if len(part) > 1:
            at = slice(2 * place * rows, 2 * (place + len(part)) * rows)
            factors, place = (gate_factor[at], up_factor[at]), 0
        d_both[part], terms = ffn_back(token, grads, *factors, place, weight_down, weight_in)
        token = zero_of(terms[0]).reshape(1)
        for i, p in enumerate(part):
            keep[p], send[p] = terms[2 * i], terms[2 * i + 1]
    d_normed_ffn = plane_scatter(keep, send)
    in_term = in_grad(n_blocks, [d_both[(0,)], d_both[(1, 2)], d_both[(3,)]], tile)
    late = zero_of(d_normed_ffn).reshape(1)
    out_terms = ffn_out(late, hidden, weight_down, 2 * MEMBERS)
    output = (residual + plane_scatter(out_terms[::2], out_terms[1::2])).astype(bf16)

    def z_sum(term):
        return lax.psum_scatter(term, "z", scatter_dimension=0, tiled=True)

    down_sum = z_sum(down_term)
    in_sum = z_sum(in_term)

    d_residual = cotangent.astype(f32) + norm_back(d_normed_ffn, residual, scale_two)
    d_attn = d_residual.astype(bf16)
    d_mixed = jnp.einsum("td,cd->tc", d_attn, weight_out, preferred_element_type=f32).astype(bf16)
    d_query, kv_terms = attend_back(
        index, queries, gathered, d_mixed, bias.transpose(0, 2, 1)
    )
    d_query = d_query.reshape(rows, HQ, HEAD)
    kv_terms = kv_terms.reshape(MEMBERS, 2, rows, 2 * HK * HEAD)
    d_pairs = plane_scatter_stacked(kv_terms[:, 0], kv_terms[:, 1])
    d_pairs = d_pairs.reshape(rows, HK, 2, HEAD)
    d_key = d_pairs[:, :, 0]
    d_value = d_pairs[:, :, 1].reshape(rows, HK * HEAD)
    d_query_normed = rotate_back(d_query, angles)
    d_key_normed = rotate_back(d_key, angles)
    q_gain_term = jnp.sum(d_query_normed * query_raw * query_scale, axis=(0, 1))
    k_gain_term = jnp.sum(d_key_normed * key_raw * key_scale, axis=(0, 1))
    d_query_raw = norm_back(d_query_normed * gain_query, query_raw, query_scale)
    d_key_raw = norm_back(d_key_normed * gain_key, key_raw, key_scale)
    d_projected = jnp.concatenate(
        [
            d_query_raw.reshape(rows, HQ * HEAD),
            d_key_raw.reshape(rows, HK * HEAD),
            d_value,
            jnp.zeros((rows, width - qkv), f32),
        ],
        axis=1,
    ).astype(bf16)
    d_normed = jnp.einsum("tc,dc->td", d_projected, weight_qkv, preferred_element_type=f32)
    input_grad = (d_residual + norm_back(d_normed, x_float, scale_one)).astype(bf16)

    def both(mine):
        other = swapped(mine, "x")
        low = jnp.where(ctx == 0, mine, other)
        high = jnp.where(ctx == 0, other, mine)
        return low, high

    def summed(keep, send):
        count, seqs_, rows_, half_ = keep.shape
        mine = plane_scatter_stacked(
            keep.reshape(count, seqs_ * rows_, half_), send.reshape(count, seqs_ * rows_, half_)
        ).astype(bf16)
        mine = lax.psum_scatter(mine, "z", scatter_dimension=0, tiled=True)
        return jnp.concatenate(both(mine), axis=1).astype(f32)

    def placed(total):
        moved = lax.all_to_all(
            total.reshape(MEMBERS, part_rows, 2 * share),
            MEMBER,
            split_axis=0,
            concat_axis=0,
            tiled=True,
        )
        low, high = both(moved)
        whole = jnp.stack([low, high]).reshape(2, MEMBERS, part_rows, 2, seqs, piece)
        return whole.transpose(3, 2, 4, 1, 0, 5).reshape(2, part_rows, ff).astype(f32)

    gate_raw, up_raw = placed(in_sum)
    ffn_norm_grad = jnp.sum(
        gate_raw * w_gate.astype(f32) + up_raw * w_up.astype(f32), axis=1
    )
    down_grad = jnp.concatenate(both(down_sum), axis=0).astype(f32)
    out_grad = summed(*gradient_terms(where, mixed, d_attn))
    gain_terms = jnp.stack([q_gain_term, k_gain_term]).reshape(2, -1, gain_width)
    gain_terms = gain_terms.transpose(1, 0, 2).reshape(seqs, MEMBERS, 1, 2 * gain_width)
    gain_terms = jnp.pad(gain_terms, ((0, 0), (0, 0), (0, 0), (0, LANES - 2 * gain_width)))
    qkv_all = summed(*gradient_terms(where, normed, d_projected, gain_terms))
    qkv_raw = qkv_all[:, :qkv]
    gain_grads = qkv_all[0, qkv:]
    attn_norm_grad = jnp.sum(qkv_raw * w_qkv.astype(f32), axis=1)
    return (
        output,
        input_grad,
        attn_norm_grad,
        qkv_raw * norm_one,
        gain_grads[:gain_width],
        gain_grads[gain_width : 2 * gain_width],
        out_grad,
        ffn_norm_grad,
        gate_raw * norm_two,
        up_raw * norm_two,
        down_grad,
    )


def solution(mesh):
    fsdp = mesh.shape["fsdp"]
    devices = mesh.devices.reshape(2, fsdp // MEMBERS, 2, 2)
    inner = jax.sharding.Mesh(devices, ("x", "z", "y", "c"))
    tokens = P(("x",) + FSDP, None)
    return jax.shard_map(
        shards,
        mesh=inner,
        in_specs=(
            tokens,
            tokens,
            P(),
            P(),
            P(),
            P(FSDP),
            P(FSDP, None),
            P(FSDP),
            P(FSDP),
            P(FSDP, None),
            P(FSDP),
            P(FSDP, None),
            P(FSDP, None),
            P(FSDP, None),
        ),
        out_specs=(
            tokens,
            tokens,
            P(FSDP),
            P(FSDP, None),
            P(FSDP),
            P(FSDP),
            P(FSDP, None),
            P(FSDP),
            P(FSDP, None),
            P(FSDP, None),
            P(FSDP, None),
        ),
        check_vma=False,
    )
```
